512 devices in a mesh: blk: 32 (over y_hi, x, core), tp: 16 (over z, y_lo).
Axes of the slice: x: 4, y: 8 (y_hi: 4, y_lo: 2; y = y_hi * 2 + y_lo), z: 8, core: 2. Of those that a mesh axis runs over, the one named last changes fastest.
Arguments:
- tokens: bfloat16 [131072, 896], P(('blk', 'tp')), may hold values from -6 to 6
- cotangent: bfloat16 [131072, 896], P(('blk', 'tp')), may hold values from -0.59765625 to 0.59765625
- weights: bfloat16 [32, 2432, 3, 896], P('blk', 'tp'), may hold values from -6 to 6
- first_moment: bfloat16 [32, 2432, 3, 896], P('blk', 'tp'), may hold values from -0.1796875 to 0.1796875
- second_moment: bfloat16 [32, 2432, 3, 896], P('blk', 'tp'), may hold values from 0.0009994507 to 0.0099487305
Outputs:
- averaged: float32 [32, 2432, 3, 896], P('blk', 'tp')
The draws below stay inside these ranges and needn't reach their ends.
All inputs are finite; a program needn't handle non-finite values.
Results may differ from the reference program's by a relative error of at most 0.0003.
Values may be sent and summed in bfloat16 or wider, within the bound.
A program may use at most 64 MiB of HBM per device.

```python
import math
import jax
import jax.numpy as jnp
from jax import lax

D = 896
TOK_DEV = 256
STEP = 10
FFW = 2432
REPLICAS = 32
TOKENS = 131072
N_BLK = 32
N_TP = 16


def block_levels(stream_key, shape, cuts, low, largest):
    loudness = 1.0
    for position, blocks in cuts:
        draws = jax.random.uniform(jax.random.fold_in(jax.random.fold_in(stream_key, 6), position), (blocks,), jnp.float32, low / len(cuts), largest / len(cuts))
        loudness = loudness * jnp.repeat(jnp.exp(draws), shape[position] // blocks).reshape((-1,) + (1,) * (len(shape) - 1 - position))
    return loudness


def bell_draw(stream_key, extent, width, most, cuts=(), held_as=jnp.bfloat16):
    array = jax.random.normal(stream_key, extent, jnp.float32) * width
    if len(cuts) > 0:
        array = block_levels(stream_key, extent, cuts, -0.22, 0.18) * array
    return jnp.clip(array, min=-most, max=most).astype(held_as)


def setup_inputs(seed: int = 0) -> dict:
    key_of = jax.random.split(jax.random.key(seed), 6)
    tokens = bell_draw(key_of[0], (TOKENS, D), 1.0, 6.0, ((0, 512),))
    cotangent = bell_draw(key_of[1], (TOKENS, D), 0.1, 0.59765625, ((0, 512),))
    weights = bell_draw(key_of[2], (REPLICAS, FFW, 3, D), 1.0, 6.0, ((0, 32), (1, 16)))
    first_moment = bell_draw(key_of[3], (REPLICAS, FFW, 3, D), 0.03, 0.1796875, ((0, 32), (1, 16)))
    second_moment = jnp.clip(jnp.exp(math.log(0.0099487305) - 2.2979944 * jax.random.uniform(key_of[4], (REPLICAS, FFW, 3, D), jnp.float32) ** block_levels(key_of[4], (REPLICAS, FFW, 3, D), ((0, 32), (1, 16)), -0.2, 0.2)), 0.0009994507, 0.0099487305).astype(jnp.bfloat16)
    return dict(tokens=tokens, cotangent=cotangent, weights=weights, first_moment=first_moment, second_moment=second_moment)


def row_terms(xs, grads_out, rows):
    width_scale = D ** (-0.5)
    hidden_scale = FFW ** (-0.5)
    gate = jnp.dot(xs, rows[:, 0, :].T, preferred_element_type=jnp.float32) * width_scale
    upper = jnp.dot(xs, rows[:, 1, :].T, preferred_element_type=jnp.float32) * width_scale
    sigma = jax.nn.sigmoid(gate)
    swish = gate * sigma
    hidden = (swish * upper).astype(jnp.bfloat16)
    back = jnp.dot(grads_out, rows[:, 2, :].T, preferred_element_type=jnp.float32) * hidden_scale
    dgate = (back * upper * sigma * (1.0 + gate * (1.0 - sigma))).astype(jnp.bfloat16)
    dupper = (back * swish).astype(jnp.bfloat16)
    grad_gate = jnp.dot(dgate.T, xs, preferred_element_type=jnp.float32) * width_scale
    grad_upper = jnp.dot(dupper.T, xs, preferred_element_type=jnp.float32) * width_scale
    grad_down = jnp.dot(hidden.T, grads_out, preferred_element_type=jnp.float32) * hidden_scale
    return jnp.stack([grad_gate, grad_upper, grad_down], axis=1)

def reference(tokens, cotangent, weights, first_moment, second_moment):
    token_blocks = tokens.reshape(N_BLK, N_TP * TOK_DEV, D)
    cot_blocks = cotangent.reshape(N_BLK, N_TP * TOK_DEV, D)

    def replica(packed):
        return row_terms(packed[0], packed[1], packed[2])
    grads = lax.map(replica, (token_blocks, cot_blocks, weights))
    moment_one = 0.9 * first_moment.astype(jnp.float32) + 0.1 * grads
    moment_two = 0.95 * second_moment.astype(jnp.float32) + 0.05 * grads * grads
    correct_one = 1.0 - 0.9 ** STEP
    correct_two = 1.0 - 0.95 ** STEP
    master = weights.astype(jnp.float32)
    step_size = moment_one / correct_one / (jnp.sqrt(moment_two / correct_two) + 1e-08)
    updated = master - 0.1 * (step_size + 0.1 * master)
    return (jnp.roll(updated, 1, axis=0) + updated + jnp.roll(updated, -1, axis=0)) / 3.0
```

```python
import functools

import jax
import jax.numpy as jnp
from jax import lax
from jax.experimental import pallas as pl
from jax.experimental.pallas import tpu as pltpu
from jax.sharding import PartitionSpec as P

STEP = 10
MESH = pl.DeviceIdType.MESH
LINK = jnp.bfloat16
NEAR = (((1,), (1,)), ((), ()))


def kernel(
    n_blk,
    n_tp,
    hidden_scale,
    tok,
    cot,
    w,
    fm,
    sm,
    out,
    xs,
    gs,
    wb,
    wn,
    fmv,
    smv,
    acc,
    gsend,
    grecv,
    ssend,
    srecv,
    local_sem,
    x_send,
    x_recv,
    g_send,
    g_recv,
    w_send,
    w_recv,
    p_send,
    p_recv,
    s_send,
    s_recv,
):
    b, t = lax.axis_index("blk"), lax.axis_index("tp")
    units, width = w.shape[1], w.shape[2]
    width_scale = width ** (-0.5)
    scales = (width_scale, width_scale, hidden_scale)
    right = {"blk": b, "tp": lax.rem(t + 2, n_tp)}
    left = {"blk": b, "tp": lax.rem(t + n_tp - 2, n_tp)}
    partner = {"blk": b, "tp": t + 1 - 2 * lax.rem(t, 2)}
    following = {"blk": lax.rem(b + 1, n_blk), "tp": t}
    previous = {"blk": lax.rem(b + n_blk - 1, n_blk), "tp": t}

    def remote(src, dst, send, recv, device):
        return pltpu.make_async_remote_copy(
            src_ref=src,
            dst_ref=dst,
            send_sem=send,
            recv_sem=recv,
            device_id=device,
            device_id_type=MESH,
        )

    local = [
        pltpu.make_async_copy(src, dst, local_sem.at[i])
        for i, (src, dst) in enumerate(
            ((tok, xs.at[0]), (cot, gs.at[0]), (w, wb.at[0]), (fm, fmv), (sm, smv))
        )
    ]
    for copy in local:
        copy.start()

    barrier = pltpu.get_barrier_semaphore()
    for device in (right, left, partner, following, previous):
        pl.semaphore_signal(barrier, inc=1, device_id=device, device_id_type=MESH)
    pl.semaphore_wait(barrier, 5)

    def forward_x(src, dst, device):
        return remote(src, xs.at[dst], x_send.at[dst], x_recv.at[dst], device)

    def forward_g(src, dst, device):
        return remote(src, gs.at[dst], g_send.at[dst], g_recv.at[dst], device)

    moves = {}
    moves["x", 1] = forward_x(tok, 1, right)
    moves["g", 2] = forward_g(cot, 2, left)
    moves["g", 1] = forward_g(cot, 1, right)
    moves["x", 2] = forward_x(tok, 2, left)
    for move in moves.values():
        move.start()
    w_moves = [
        remote(w, wb.at[1], w_send.at[0], w_recv.at[0], partner),
        remote(w, wn.at[0], w_send.at[1], w_recv.at[1], following),
        remote(w, wn.at[1], w_send.at[2], w_recv.at[2], previous),
    ]
    for move in w_moves:
        move.start()

    acc[...] = jnp.zeros_like(acc)

    def compute(slot, half):
        x, g = xs[slot], gs[slot]

        def near(rows, data):
            return lax.dot_general(rows, data, NEAR, preferred_element_type=jnp.float32)

        gate = near(wb[half, 0], x) * width_scale
        upper = near(wb[half, 1], x) * width_scale
        back = near(wb[half, 2], g) * hidden_scale
        sigma = jax.nn.sigmoid(gate)
        swish = gate * sigma
        hidden = (swish * upper).astype(jnp.bfloat16)
        dgate = (back * upper * sigma * (1.0 + gate * (1.0 - sigma))).astype(jnp.bfloat16)
        dupper = (back * swish).astype(jnp.bfloat16)
        acc[half, 0] += jnp.dot(dgate, x, preferred_element_type=jnp.float32)
        acc[half, 1] += jnp.dot(dupper, x, preferred_element_type=jnp.float32)
        acc[half, 2] += jnp.dot(hidden, g, preferred_element_type=jnp.float32)

    def both_halves(first_slot, slots):
        @pl.loop(0, 2 * slots)
        def _(i):
            compute(first_slot + i // 2, 1 - i % 2)

    for copy in local:
        copy.wait()
    compute(0, 0)
    for step in (1, 2, 3):
        r, l = 2 * step - 1, 2 * step
        order = (("x", r), ("g", l), ("g", r), ("x", l))
        for kind, slot in order:
            moves[kind, slot].wait_recv()
            if step < 3:
                target, device = slot + 2, right if slot == r else left
            elif (kind, slot) == ("x", r):
                target, device = 7, right
            elif (kind, slot) == ("g", l):
                target, device = 7, left
            else:
                continue
            if kind == "x":
                moves[kind, target] = forward_x(xs.at[slot], target, device)
            else:
                moves[kind, target] = forward_g(gs.at[slot], target, device)
            moves[kind, target].start()
        if step == 1:
            w_moves[0].wait_recv()
            compute(0, 1)
        both_halves(r, 2)
    moves["x", 7].wait_recv()
    moves["g", 7].wait_recv()
    compute(7, 1)

    cut = units // 32 * 16 + 16
    pieces = [(m, pl.ds(lo, n)) for m in range(3) for lo, n in ((0, cut), (cut, units - cut))]
    p_moves = []
    for i, (m, rows) in enumerate(pieces):
        gsend[m, rows] = acc[1, m, rows].astype(LINK)
        p_moves.append(
            remote(gsend.at[m, rows], grecv.at[m, rows], p_send.at[i], p_recv.at[i], partner)
        )
        p_moves[-1].start()
    compute(7, 0)
    w_moves[1].wait_recv()
    w_moves[2].wait_recv()

    correct_one = 1.0 - 0.9**STEP
    correct_two = 1.0 - 0.95**STEP
    s_moves = []

    def adam(i):
        m, rows = pieces[i]
        p_moves[i].wait_recv()
        grad = (acc[0, m, rows] + grecv[m, rows].astype(jnp.float32)) * scales[m]
        one = 0.9 * fmv[m, rows].astype(jnp.float32) + 0.1 * grad
        two = 0.95 * smv[m, rows].astype(jnp.float32) + 0.05 * grad * grad
        step = one / correct_one / (jnp.sqrt(two / correct_two) + 1e-08)
        acc[0, m, rows] = step
        ssend[m, rows] = step.astype(LINK)
        for j, device in enumerate((following, previous)):
            move = remote(
                ssend.at[m, rows],
                srecv.at[j, m, rows],
                s_send.at[j, i],
                s_recv.at[j, i],
                device,
            )
            move.start()
            s_moves.append(move)

    def average(i):
        m, rows = pieces[i]
        s_moves[2 * i].wait_recv()
        s_moves[2 * i + 1].wait_recv()
        f32 = jnp.float32
        steps = acc[0, m, rows] + srecv[0, m, rows].astype(f32) + srecv[1, m, rows].astype(f32)
        rest = wb[0, m, rows].astype(f32) + wn[0, m, rows].astype(f32) + wn[1, m, rows].astype(f32)
        out[m, rows] = (0.99 * rest - 0.1 * steps) / 3.0

    lag = 2
    for i in range(len(pieces) + lag):
        if i < len(pieces):
            adam(i)
        if i >= lag:
            average(i - lag)
    for move in list(moves.values()) + w_moves + p_moves + s_moves:
        move.wait_send()


def on_device(n_blk, n_tp, tokens, cotangent, weights, first_moment, second_moment):
    rows, width = tokens.shape
    units = weights.shape[1]
    shape = (3, units, width)
    bf16, f32 = jnp.bfloat16, jnp.float32
    slots = n_tp // 2
    pieces = 6
    by_kind = [a[0].transpose(1, 0, 2) for a in (weights, first_moment, second_moment)]
    dma = pltpu.SemaphoreType.DMA
    averaged = pl.pallas_call(
        functools.partial(kernel, n_blk, n_tp, (units * n_tp) ** (-0.5)),
        out_shape=jax.ShapeDtypeStruct(shape, f32),
        in_specs=[pl.BlockSpec(memory_space=pl.ANY)] * 5,
        out_specs=pl.BlockSpec(memory_space=pltpu.VMEM),
        scratch_shapes=[
            pltpu.VMEM((slots, rows, width), bf16),
            pltpu.VMEM((slots, rows, width), bf16),
            pltpu.VMEM((2,) + shape, bf16),
            pltpu.VMEM((2,) + shape, bf16),
            pltpu.VMEM(shape, bf16),
            pltpu.VMEM(shape, bf16),
            pltpu.VMEM((2,) + shape, f32),
            pltpu.VMEM(shape, LINK),
            pltpu.VMEM(shape, LINK),
            pltpu.VMEM(shape, LINK),
            pltpu.VMEM((2,) + shape, LINK),
            dma((5,)),
            dma((slots,)),
            dma((slots,)),
            dma((slots,)),
            dma((slots,)),
            dma((3,)),
            dma((3,)),
            dma((pieces,)),
            dma((pieces,)),
            dma((2, pieces)),
            dma((2, pieces)),
        ],
        compiler_params=pltpu.CompilerParams(
            collective_id=0, has_side_effects=True, vmem_limit_bytes=60 << 20
        ),
    )(tokens, cotangent, *by_kind)
    return averaged.transpose(1, 0, 2)[None]


def solution(mesh):
    in_specs = (
        P(("blk", "tp"), None),
        P(("blk", "tp"), None),
        P("blk", "tp", None, None),
        P("blk", "tp", None, None),
        P("blk", "tp", None, None),
    )
    out_specs = P("blk", "tp", None, None)
    return jax.shard_map(
        functools.partial(on_device, mesh.shape["blk"], mesh.shape["tp"]),
        mesh=mesh,
        in_specs=in_specs,
        out_specs=out_specs,
        check_vma=False,
    )
```

```python
import functools

import jax
import jax.numpy as jnp
from jax import lax
from jax.experimental import pallas as pl
from jax.experimental.pallas import tpu as pltpu
from jax.sharding import PartitionSpec as P

STEP = 10
ROW = 8
PARTS = 3
MESH = pl.DeviceIdType.MESH
LINK = jnp.bfloat16
NEAR = (((1,), (1,)), ((), ()))


def cuts(units):
    size = units // PARTS // 16 * 16
    return [(i * size, size if i < PARTS - 1 else units - i * size) for i in range(PARTS)]


def kernel(
    n_blk,
    n_tp,
    hidden_scale,
    tok,
    cot,
    w,
    fm,
    sm,
    out,
    xs,
    gs,
    wb,
    wn,
    fmv,
    smv,
    acc,
    gsend,
    grecv,
    ssend,
    srecv,
    relayed,
    local_sem,
    x_send,
    x_recv,
    g_send,
    g_recv,
    w_send,
    w_recv,
    p_send,
    p_recv,
    s_send,
    s_recv,
    r_send,
    r_recv,
):
    b, t = lax.axis_index("blk"), lax.axis_index("tp")
    units, width = w.shape[1], w.shape[2]
    width_scale = width ** (-0.5)
    scales = (width_scale, width_scale, hidden_scale)
    right = {"blk": b, "tp": lax.rem(t + 2, n_tp)}
    left = {"blk": b, "tp": lax.rem(t + n_tp - 2, n_tp)}
    partner = {"blk": b, "tp": t + 1 - 2 * lax.rem(t, 2)}
    following = {"blk": lax.rem(b + 1, n_blk), "tp": t}
    previous = {"blk": lax.rem(b + n_blk - 1, n_blk), "tp": t}

    place = lax.rem(b, ROW)
    even = lax.rem(t, 2) == 0
    last = jnp.logical_and(place == ROW - 1, even)
    first = jnp.logical_and(place == 0, even)
    up = {"blk": lax.rem(b + ROW, n_blk), "tp": t}
    down = {"blk": lax.rem(b + n_blk - ROW, n_blk), "tp": t}
    across = {"blk": lax.rem(b + n_blk + ROW - 1 - 2 * place, n_blk), "tp": t}

    def remote(src, dst, send, recv, device):
        return pltpu.make_async_remote_copy(
            src_ref=src,
            dst_ref=dst,
            send_sem=send,
            recv_sem=recv,
            device_id=device,
            device_id_type=MESH,
        )

    local = [
        pltpu.make_async_copy(src, dst, local_sem.at[i])
        for i, (src, dst) in enumerate(
            ((tok, xs.at[0]), (cot, gs.at[0]), (w, wb.at[0]), (fm, fmv), (sm, smv))
        )
    ]
    for copy in local:
        copy.start()

    barrier = pltpu.get_barrier_semaphore()
    for device in (right, left, partner, following, previous):
        pl.semaphore_signal(barrier, inc=1, device_id=device, device_id_type=MESH)
    wraps_round = jnp.logical_or(last, first)

    @pl.when(jnp.logical_not(wraps_round))
    def _():
        pl.semaphore_wait(barrier, 5)

    @pl.when(wraps_round)
    def _():
        for device in (up, down, across):
            pl.semaphore_signal(barrier, inc=1, device_id=device, device_id_type=MESH)
        pl.semaphore_wait(barrier, 8)

    def forward_x(src, dst, device):
        return remote(src, xs.at[dst], x_send.at[dst], x_recv.at[dst], device)

    def forward_g(src, dst, device):
        return remote(src, gs.at[dst], g_send.at[dst], g_recv.at[dst], device)

    moves = {}
    moves["x", 1] = forward_x(tok, 1, right)
    moves["g", 2] = forward_g(cot, 2, left)
    moves["g", 1] = forward_g(cot, 1, right)
    moves["x", 2] = forward_x(tok, 2, left)
    for move in moves.values():
        move.start()
    w_moves = [
        remote(w, wb.at[1], w_send.at[0], w_recv.at[0], partner),
        remote(w, wn.at[0], w_send.at[1], w_recv.at[1], following),
        remote(w, wn.at[1], w_send.at[2], w_recv.at[2], previous),
    ]
    for move in w_moves:
        move.start()

    acc[...] = jnp.zeros_like(acc)

    def compute(slot, half):
        x, g = xs[slot], gs[slot]

        def near(rows, data):
            return lax.dot_general(rows, data, NEAR, preferred_element_type=jnp.float32)

        gate = near(wb[half, 0], x) * width_scale
        upper = near(wb[half, 1], x) * width_scale
        back = near(wb[half, 2], g) * hidden_scale
        sigma = jax.nn.sigmoid(gate)
        swish = gate * sigma
        hidden = (swish * upper).astype(jnp.bfloat16)
        dgate = (back * upper * sigma * (1.0 + gate * (1.0 - sigma))).astype(jnp.bfloat16)
        dupper = (back * swish).astype(jnp.bfloat16)
        acc[half, 0] += jnp.dot(dgate, x, preferred_element_type=jnp.float32)
        acc[half, 1] += jnp.dot(dupper, x, preferred_element_type=jnp.float32)
        acc[half, 2] += jnp.dot(hidden, g, preferred_element_type=jnp.float32)

    def both_halves(first_slot, slots):
        @pl.loop(0, 2 * slots)
        def _(i):
            compute(first_slot + i // 2, 1 - i % 2)

    for copy in local:
        copy.wait()
    compute(0, 0)
    for step in (1, 2, 3):
        r, l = 2 * step - 1, 2 * step
        order = (("x", r), ("g", l), ("g", r), ("x", l))
        for kind, slot in order:
            moves[kind, slot].wait_recv()
            if step < 3:
                target, device = slot + 2, right if slot == r else left
            elif (kind, slot) == ("x", r):
                target, device = 7, right
            elif (kind, slot) == ("g", l):
                target, device = 7, left
            else:
                continue
            if kind == "x":
                moves[kind, target] = forward_x(xs.at[slot], target, device)
            else:
                moves[kind, target] = forward_g(gs.at[slot], target, device)
            moves[kind, target].start()
        if step == 1:
            w_moves[0].wait_recv()
            compute(0, 1)
        both_halves(r, 2)
    moves["x", 7].wait_recv()
    moves["g", 7].wait_recv()
    compute(7, 1)

    pieces = [(m, pl.ds(lo, n)) for m in range(3) for lo, n in cuts(units)]
    p_moves = []
    for i, (m, rows) in enumerate(pieces):
        gsend[m, rows] = acc[1, m, rows].astype(LINK)
        p_moves.append(
            remote(gsend.at[m, rows], grecv.at[m, rows], p_send.at[i], p_recv.at[i], partner)
        )
        p_moves[-1].start()
    compute(7, 0)
    w_moves[1].wait_recv()
    w_moves[2].wait_recv()

    correct_one = 1.0 - 0.9**STEP
    correct_two = 1.0 - 0.95**STEP
    s_moves = []

    def adam(i):
        m, rows = pieces[i]
        p_moves[i].wait_recv()
        grad = (acc[0, m, rows] + grecv[m, rows].astype(jnp.float32)) * scales[m]
        one = 0.9 * fmv[m, rows].astype(jnp.float32) + 0.1 * grad
        two = 0.95 * smv[m, rows].astype(jnp.float32) + 0.05 * grad * grad
        step = one / correct_one / (jnp.sqrt(two / correct_two) + 1e-08)
        acc[0, m, rows] = step
        ssend[m, rows] = step.astype(LINK)
        ends = ((following, last, up), (previous, first, down))
        for j, (device, wraps, relay) in enumerate(ends):
            move = remote(
                ssend.at[m, rows],
                srecv.at[j, m, rows],
                s_send.at[j, i],
                s_recv.at[j, i],
                device,
            )
            s_moves.append(move)
            pl.when(jnp.logical_not(wraps))(move.start)
            detour = remote(
                ssend.at[m, rows],
                relayed.at[m, rows],
                s_send.at[j, i],
                r_recv.at[i],
                relay,
            )
            pl.when(wraps)(detour.start)

    def relay_on(i, j):
        m, rows = pieces[i]
        return remote(
            relayed.at[m, rows], srecv.at[j, m, rows], r_send.at[i], s_recv.at[j, i], across
        )

    def relay(i):
        m, rows = pieces[i]
        for j, (wraps, device) in enumerate(((last, up), (first, down))):

            @pl.when(wraps)
            def _(j=j, device=device):
                remote(
                    relayed.at[m, rows], relayed.at[m, rows], r_send.at[i], r_recv.at[i], device
                ).wait_recv()
                relay_on(i, j).start()

    def average(i):
        m, rows = pieces[i]
        s_moves[2 * i].wait_recv()
        s_moves[2 * i + 1].wait_recv()
        f32 = jnp.float32
        steps = acc[0, m, rows] + srecv[0, m, rows].astype(f32) + srecv[1, m, rows].astype(f32)
        rest = wb[0, m, rows].astype(f32) + wn[0, m, rows].astype(f32) + wn[1, m, rows].astype(f32)
        out[m, rows] = 0.99 * rest - 0.1 * steps

    for i in range(len(pieces) + 4):
        if i < len(pieces):
            adam(i)
        if 0 <= i - 2 < len(pieces):
            relay(i - 2)
        if i >= 4:
            average(i - 4)
    for move in list(moves.values()) + w_moves + p_moves + s_moves:
        move.wait_send()

    @pl.when(wraps_round)
    def _():
        for i in range(len(pieces)):
            relay_on(i, 0).wait_send()


def on_device(n_blk, n_tp, tokens, cotangent, weights, first_moment, second_moment):
    rows, width = tokens.shape
    units = weights.shape[1]
    shape = (3, units, width)
    bf16, f32 = jnp.bfloat16, jnp.float32
    slots = n_tp // 2
    pieces = 3 * PARTS
    by_kind = [a[0].transpose(1, 0, 2) for a in (weights, first_moment, second_moment)]
    dma = pltpu.SemaphoreType.DMA
    arrays = [pltpu.with_memory_space_constraint(a, pltpu.HBM) for a in (tokens, cotangent, *by_kind)]
    total = pl.pallas_call(
        functools.partial(kernel, n_blk, n_tp, (units * n_tp) ** (-0.5)),
        out_shape=jax.ShapeDtypeStruct(shape, f32),
        in_specs=[pl.BlockSpec(memory_space=pltpu.HBM)] * 5,
        out_specs=pl.BlockSpec(memory_space=pltpu.VMEM),
        scratch_shapes=[
            pltpu.VMEM((slots, rows, width), bf16),
            pltpu.VMEM((slots, rows, width), bf16),
            pltpu.VMEM((2,) + shape, bf16),
            pltpu.VMEM((2,) + shape, bf16),
            pltpu.VMEM(shape, bf16),
            pltpu.VMEM(shape, bf16),
            pltpu.VMEM((2,) + shape, f32),
            pltpu.VMEM(shape, LINK),
            pltpu.VMEM(shape, LINK),
            pltpu.VMEM(shape, LINK),
            pltpu.VMEM((2,) + shape, LINK),
            pltpu.VMEM(shape, LINK),
            dma((5,)),
            dma((slots,)),
            dma((slots,)),
            dma((slots,)),
            dma((slots,)),
            dma((3,)),
            dma((3,)),
            dma((pieces,)),
            dma((pieces,)),
            dma((2, pieces)),
            dma((2, pieces)),
            dma((pieces,)),
            dma((pieces,)),
        ],
        compiler_params=pltpu.CompilerParams(
            collective_id=0, has_side_effects=True, vmem_limit_bytes=36 << 20
        ),
    )(*arrays)
    return (total / 3.0).transpose(1, 0, 2)[None]


def solution(mesh):
    in_specs = (
        P(("blk", "tp"), None),
        P(("blk", "tp"), None),
        P("blk", "tp", None, None),
        P("blk", "tp", None, None),
        P("blk", "tp", None, None),
    )
    out_specs = P("blk", "tp", None, None)
    return jax.shard_map(
        functools.partial(on_device, mesh.shape["blk"], mesh.shape["tp"]),
        mesh=mesh,
        in_specs=in_specs,
        out_specs=out_specs,
        check_vma=False,
    )
```

```python
import functools

import jax
import jax.numpy as jnp
from jax import lax
from jax.experimental import pallas as pl
from jax.experimental.pallas import tpu as pltpu
from jax.sharding import PartitionSpec as P

STEP = 10
ROW = 8
PARTS = 3
LATE = 32
MESH = pl.DeviceIdType.MESH
LINK = jnp.bfloat16
NEAR = (((1,), (1,)), ((), ()))


def cuts(units):
    size = units // PARTS // 16 * 16
    return [(i * size, size if i < PARTS - 1 else units - i * size) for i in range(PARTS)]


def kernel(
    n_blk,
    n_tp,
    hidden_scale,
    tok,
    cot,
    w,
    fm,
    sm,
    out,
    xs,
    gs,
    lx,
    lg,
    wb,
    wn,
    fmv,
    smv,
    acc,
    gsend,
    grecv,
    ssend,
    srecv,
    relayed,
    local_sem,
    x_send,
    x_recv,
    g_send,
    g_recv,
    lx_send,
    lx_recv,
    lg_send,
    lg_recv,
    w_send,
    w_recv,
    p_send,
    p_recv,
    s_send,
    s_recv,
    r_send,
    r_recv,
):
    b, t = lax.axis_index("blk"), lax.axis_index("tp")
    units, width = w.shape[1], w.shape[2]
    width_scale = width ** (-0.5)
    soon, late = pl.ds(0, tok.shape[0] - LATE), pl.ds(tok.shape[0] - LATE, LATE)
    scales = (width_scale, width_scale, hidden_scale)
    right = {"blk": b, "tp": lax.rem(t + 2, n_tp)}
    left = {"blk": b, "tp": lax.rem(t + n_tp - 2, n_tp)}
    partner = {"blk": b, "tp": t + 1 - 2 * lax.rem(t, 2)}
    following = {"blk": lax.rem(b + 1, n_blk), "tp": t}
    previous = {"blk": lax.rem(b + n_blk - 1, n_blk), "tp": t}

    place = lax.rem(b, ROW)
    even = lax.rem(t, 2) == 0
    last = jnp.logical_and(place == ROW - 1, even)
    first = jnp.logical_and(place == 0, even)
    up = {"blk": lax.rem(b + ROW, n_blk), "tp": t}
    down = {"blk": lax.rem(b + n_blk - ROW, n_blk), "tp": t}
    across = {"blk": lax.rem(b + n_blk + ROW - 1 - 2 * place, n_blk), "tp": t}

    def remote(src, dst, send, recv, device):
        return pltpu.make_async_remote_copy(
            src_ref=src,
            dst_ref=dst,
            send_sem=send,
            recv_sem=recv,
            device_id=device,
            device_id_type=MESH,
        )

    local = [
        pltpu.make_async_copy(src, dst, local_sem.at[i])
        for i, (src, dst) in enumerate(
            (
                (tok.at[soon], xs.at[0]),
                (cot.at[soon], gs.at[0]),
                (w, wb.at[0]),
                (fm, fmv),
                (sm, smv),
                (tok.at[late], lx.at[pl.ds(0, LATE)]),
                (cot.at[late], lg.at[pl.ds(0, LATE)]),
            )
        )
    ]
    for copy in local:
        copy.start()

    barrier = pltpu.get_barrier_semaphore()
    for device in (right, left, partner, following, previous):
        pl.semaphore_signal(barrier, inc=1, device_id=device, device_id_type=MESH)
    wraps_round = jnp.logical_or(last, first)

    @pl.when(jnp.logical_not(wraps_round))
    def _():
        pl.semaphore_wait(barrier, 5)

    @pl.when(wraps_round)
    def _():
        for device in (up, down, across):
            pl.semaphore_signal(barrier, inc=1, device_id=device, device_id_type=MESH)
        pl.semaphore_wait(barrier, 8)

    def forward_x(src, dst, device):
        return remote(src, xs.at[dst], x_send.at[dst], x_recv.at[dst], device)

    def forward_g(src, dst, device):
        return remote(src, gs.at[dst], g_send.at[dst], g_recv.at[dst], device)

    def of_slot(slot):
        return pl.ds(2 * LATE * slot, 2 * LATE)

    def forward_late(kind, src, dst, device):
        held, send, recv = (lx, lx_send, lx_recv) if kind == "x" else (lg, lg_send, lg_recv)
        return remote(held.at[of_slot(src)], held.at[of_slot(dst)], send.at[dst], recv.at[dst], device)

    moves = {}
    moves["x", 1] = forward_x(tok.at[soon], 1, right)
    moves["g", 2] = forward_g(cot.at[soon], 2, left)
    moves["g", 1] = forward_g(cot.at[soon], 1, right)
    moves["x", 2] = forward_x(tok.at[soon], 2, left)
    other = pl.ds(LATE, LATE)
    lates = {
        ("x", 0): remote(tok.at[late], lx.at[other], lx_send.at[0], lx_recv.at[0], partner),
        ("g", 0): remote(cot.at[late], lg.at[other], lg_send.at[0], lg_recv.at[0], partner),
    }
    for move in list(moves.values()) + list(lates.values()):
        move.start()
    w_moves = [
        remote(w, wb.at[1], w_send.at[0], w_recv.at[0], partner),
        remote(w, wn.at[0], w_send.at[1], w_recv.at[1], following),
        remote(w, wn.at[1], w_send.at[2], w_recv.at[2], previous),
    ]
    for move in w_moves:
        move.start()

    acc[...] = jnp.zeros_like(acc)

    def compute(slot, half):
        add_terms(xs[slot], gs[slot], half)

    def add_terms(x, g, half):

        def near(rows, data):
            return lax.dot_general(rows, data, NEAR, preferred_element_type=jnp.float32)

        gate = near(wb[half, 0], x) * width_scale
        upper = near(wb[half, 1], x) * width_scale
        back = near(wb[half, 2], g) * hidden_scale
        sigma = jax.nn.sigmoid(gate)
        swish = gate * sigma
        hidden = (swish * upper).astype(jnp.bfloat16)
        dgate = (back * upper * sigma * (1.0 + gate * (1.0 - sigma))).astype(jnp.bfloat16)
        dupper = (back * swish).astype(jnp.bfloat16)
        acc[half, 0] += jnp.dot(dgate, x, preferred_element_type=jnp.float32)
        acc[half, 1] += jnp.dot(dupper, x, preferred_element_type=jnp.float32)
        acc[half, 2] += jnp.dot(hidden, g, preferred_element_type=jnp.float32)

    def both_halves(first_slot, slots):
        @pl.loop(0, 2 * slots)
        def _(i):
            compute(first_slot + i // 2, 1 - i % 2)

    for copy in local:
        copy.wait()
    compute(0, 0)
    for step in (1, 2, 3):
        r, l = 2 * step - 1, 2 * step
        order = (("x", r), ("g", l), ("g", r), ("x", l))
        for kind, slot in order:
            moves[kind, slot].wait_recv()
            if step < 3:
                target, device = slot + 2, right if slot == r else left
            elif (kind, slot) == ("x", r):
                target, device = 7, right
            elif (kind, slot) == ("g", l):
                target, device = 7, left
            else:
                continue
            if kind == "x":
                moves[kind, target] = forward_x(xs.at[slot], target, device)
            else:
                moves[kind, target] = forward_g(gs.at[slot], target, device)
            moves[kind, target].start()
        if step == 3:
            for kind in ("x", "g"):
                lates[kind, 0].wait_recv()
            for kind, dst, device in (("x", 1, right), ("g", 2, left), ("g", 1, right), ("x", 2, left)):
                lates[kind, dst] = forward_late(kind, 0, dst, device)
                lates[kind, dst].start()
        if step == 1:
            w_moves[0].wait_recv()
            compute(0, 1)
        both_halves(r, 2)
    moves["x", 7].wait_recv()
    moves["g", 7].wait_recv()
    compute(7, 1)

    pieces = [(m, pl.ds(lo, n)) for m in range(3) for lo, n in cuts(units)]
    p_moves = []
    for i, (m, rows) in enumerate(pieces):
        gsend[m, rows] = acc[1, m, rows].astype(LINK)
        p_moves.append(
            remote(gsend.at[m, rows], grecv.at[m, rows], p_send.at[i], p_recv.at[i], partner)
        )
        p_moves[-1].start()
    compute(7, 0)

    def add_late(pair):
        rows = pl.ds(4 * LATE * pair, 4 * LATE)
        add_terms(lx[rows], lg[rows], 0)

    for step in (1, 2, 3):
        r, l = 2 * step - 1, 2 * step
        for kind, slot in (("x", r), ("g", l), ("g", r), ("x", l)):
            lates[kind, slot].wait_recv()
            target, device = slot + 2, right if slot == r else left
            if step == 3:
                if (kind, slot) not in (("x", r), ("g", l)):
                    continue
                target = 7
            lates[kind, target] = forward_late(kind, slot, target, device)
            lates[kind, target].start()
        add_late(step - 1)
    for kind in ("x", "g"):
        lates[kind, 7].wait_recv()
    add_late(3)
    w_moves[1].wait_recv()
    w_moves[2].wait_recv()

    correct_one = 1.0 - 0.9**STEP
    correct_two = 1.0 - 0.95**STEP
    s_moves = []

    def adam(i):
        m, rows = pieces[i]
        p_moves[i].wait_recv()
        grad = (acc[0, m, rows] + grecv[m, rows].astype(jnp.float32)) * scales[m]
        one = 0.9 * fmv[m, rows].astype(jnp.float32) + 0.1 * grad
        two = 0.95 * smv[m, rows].astype(jnp.float32) + 0.05 * grad * grad
        step = one / correct_one / (jnp.sqrt(two / correct_two) + 1e-08)
        acc[0, m, rows] = step
        ssend[m, rows] = step.astype(LINK)
        ends = ((following, last, across), (previous, first, across))
        for j, (device, wraps, relay) in enumerate(ends):
            move = remote(
                ssend.at[m, rows],
                srecv.at[j, m, rows],
                s_send.at[j, i],
                s_recv.at[j, i],
                device,
            )
            s_moves.append(move)
            pl.when(jnp.logical_not(wraps))(move.start)
            detour = remote(
                ssend.at[m, rows],
                relayed.at[m, rows],
                s_send.at[j, i],
                r_recv.at[i],
                relay,
            )
            pl.when(wraps)(detour.start)

    def relay_on(i, j, device):
        m, rows = pieces[i]
        return remote(
            relayed.at[m, rows], srecv.at[j, m, rows], r_send.at[i], s_recv.at[j, i], device
        )

    def relay(i):
        m, rows = pieces[i]
        for j, (wraps, device) in enumerate(((first, up), (last, down))):

            @pl.when(wraps)
            def _(j=j, device=device):
                remote(
                    relayed.at[m, rows], relayed.at[m, rows], r_send.at[i], r_recv.at[i], across
                ).wait_recv()
                relay_on(i, j, device).start()

    def average(i):
        m, rows = pieces[i]
        s_moves[2 * i].wait_recv()
        s_moves[2 * i + 1].wait_recv()
        f32 = jnp.float32
        steps = acc[0, m, rows] + srecv[0, m, rows].astype(f32) + srecv[1, m, rows].astype(f32)
        rest = wb[0, m, rows].astype(f32) + wn[0, m, rows].astype(f32) + wn[1, m, rows].astype(f32)
        out[m, rows] = 0.99 * rest - 0.1 * steps

    for i in range(len(pieces) + 4):
        if i < len(pieces):
            adam(i)
        if 0 <= i - 2 < len(pieces):
            relay(i - 2)
        if i >= 4:
            average(i - 4)
    for move in list(moves.values()) + list(lates.values()) + w_moves + p_moves + s_moves:
        move.wait_send()

    @pl.when(wraps_round)
    def _():
        for i in range(len(pieces)):
            relay_on(i, 0, across).wait_send()


def on_device(n_blk, n_tp, tokens, cotangent, weights, first_moment, second_moment):
    rows, width = tokens.shape
    units = weights.shape[1]
    shape = (3, units, width)
    bf16, f32 = jnp.bfloat16, jnp.float32
    slots = n_tp // 2
    pieces = 3 * PARTS
    by_kind = [a[0].transpose(1, 0, 2) for a in (weights, first_moment, second_moment)]
    dma = pltpu.SemaphoreType.DMA
    arrays = [pltpu.with_memory_space_constraint(a, pltpu.HBM) for a in (tokens, cotangent, *by_kind)]
    total = pl.pallas_call(
        functools.partial(kernel, n_blk, n_tp, (units * n_tp) ** (-0.5)),
        out_shape=jax.ShapeDtypeStruct(shape, f32),
        in_specs=[pl.BlockSpec(memory_space=pltpu.HBM)] * 5,
        out_specs=pl.BlockSpec(memory_space=pltpu.VMEM),
        scratch_shapes=[
            pltpu.VMEM((slots, rows - LATE, width), bf16),
            pltpu.VMEM((slots, rows - LATE, width), bf16),
            pltpu.VMEM((slots * 2 * LATE, width), bf16),
            pltpu.VMEM((slots * 2 * LATE, width), bf16),
            pltpu.VMEM((2,) + shape, bf16),
            pltpu.VMEM((2,) + shape, bf16),
            pltpu.VMEM(shape, bf16),
            pltpu.VMEM(shape, bf16),
            pltpu.VMEM((2,) + shape, f32),
            pltpu.VMEM(shape, LINK),
            pltpu.VMEM(shape, LINK),
            pltpu.VMEM(shape, LINK),
            pltpu.VMEM((2,) + shape, LINK),
            pltpu.VMEM(shape, LINK),
            dma((7,)),
            dma((slots,)),
            dma((slots,)),
            dma((slots,)),
            dma((slots,)),
            dma((slots,)),
            dma((slots,)),
            dma((slots,)),
            dma((slots,)),
            dma((3,)),
            dma((3,)),
            dma((pieces,)),
            dma((pieces,)),
            dma((2, pieces)),
            dma((2, pieces)),
            dma((pieces,)),
            dma((pieces,)),
        ],
        compiler_params=pltpu.CompilerParams(
            collective_id=0, has_side_effects=True, vmem_limit_bytes=36 << 20
        ),
    )(*arrays)
    return (total / 3.0).transpose(1, 0, 2)[None]


def solution(mesh):
    in_specs = (
        P(("blk", "tp"), None),
        P(("blk", "tp"), None),
        P("blk", "tp", None, None),
        P("blk", "tp", None, None),
        P("blk", "tp", None, None),
    )
    out_specs = P("blk", "tp", None, None)
    return jax.shard_map(
        functools.partial(on_device, mesh.shape["blk"], mesh.shape["tp"]),
        mesh=mesh,
        in_specs=in_specs,
        out_specs=out_specs,
        check_vma=False,
    )
```

```python
import functools

import jax
import jax.numpy as jnp
from jax import lax
from jax.experimental import pallas as pl
from jax.experimental.pallas import tpu as pltpu
from jax.sharding import PartitionSpec as P

STEP = 10
ROW = 8
PARTS = 3
LATE = 32
MESH = pl.DeviceIdType.MESH
LINK = jnp.bfloat16
NEAR = (((1,), (1,)), ((), ()))


def cuts(units):
    size = units // PARTS // 16 * 16
    return [(i * size, size if i < PARTS - 1 else units - i * size) for i in range(PARTS)]


def kernel(
    n_blk,
    n_tp,
    hidden_scale,
    tok,
    cot,
    w,
    fm,
    sm,
    out,
    xs,
    gs,
    lx,
    lg,
    wb,
    wn,
    fmv,
    smv,
    acc,
    gsend,
    grecv,
    ssend,
    srecv,
    relayed,
    local_sem,
    x_send,
    x_recv,
    g_send,
    g_recv,
    lx_send,
    lx_recv,
    lg_send,
    lg_recv,
    w_send,
    w_recv,
    p_send,
    p_recv,
    s_send,
    s_recv,
    r_send,
    r_recv,
):
    b, t = lax.axis_index("blk"), lax.axis_index("tp")
    units, width = w.shape[1], w.shape[2]
    width_scale = width ** (-0.5)
    soon, late = pl.ds(0, tok.shape[0] - LATE), pl.ds(tok.shape[0] - LATE, LATE)
    scales = (width_scale, width_scale, hidden_scale)
    right = {"blk": b, "tp": lax.rem(t + 2, n_tp)}
    left = {"blk": b, "tp": lax.rem(t + n_tp - 2, n_tp)}
    partner = {"blk": b, "tp": t + 1 - 2 * lax.rem(t, 2)}
    following = {"blk": lax.rem(b + 1, n_blk), "tp": t}
    previous = {"blk": lax.rem(b + n_blk - 1, n_blk), "tp": t}

    place = lax.rem(b, ROW)
    last, first = place == ROW - 1, place == 0
    up = {"blk": lax.rem(b + ROW, n_blk), "tp": t}
    down = {"blk": lax.rem(b + n_blk - ROW, n_blk), "tp": t}
    across = {"blk": lax.rem(b + n_blk + ROW - 1 - 2 * place, n_blk), "tp": t}

    def remote(src, dst, send, recv, device):
        return pltpu.make_async_remote_copy(
            src_ref=src,
            dst_ref=dst,
            send_sem=send,
            recv_sem=recv,
            device_id=device,
            device_id_type=MESH,
        )

    local = [
        pltpu.make_async_copy(src, dst, local_sem.at[i])
        for i, (src, dst) in enumerate(
            (
                (tok.at[soon], xs.at[0]),
                (cot.at[soon], gs.at[0]),
                (w, wb.at[0]),
                (fm, fmv),
                (sm, smv),
                (tok.at[late], lx.at[pl.ds(0, LATE)]),
                (cot.at[late], lg.at[pl.ds(0, LATE)]),
            )
        )
    ]
    for copy in local:
        copy.start()

    barrier = pltpu.get_barrier_semaphore()
    for device in (right, left, partner, following, previous):
        pl.semaphore_signal(barrier, inc=1, device_id=device, device_id_type=MESH)
    wraps_round = jnp.logical_or(last, first)

    @pl.when(jnp.logical_not(wraps_round))
    def _():
        pl.semaphore_wait(barrier, 5)

    @pl.when(wraps_round)
    def _():
        for device in (up, down, across):
            pl.semaphore_signal(barrier, inc=1, device_id=device, device_id_type=MESH)
        pl.semaphore_wait(barrier, 8)

    def forward_x(src, dst, device):
        return remote(src, xs.at[dst], x_send.at[dst], x_recv.at[dst], device)

    def forward_g(src, dst, device):
        return remote(src, gs.at[dst], g_send.at[dst], g_recv.at[dst], device)

    def of_slot(slot):
        return pl.ds(2 * LATE * slot, 2 * LATE)

    def forward_late(kind, src, dst, device):
        held, send, recv = (lx, lx_send, lx_recv) if kind == "x" else (lg, lg_send, lg_recv)
        return remote(held.at[of_slot(src)], held.at[of_slot(dst)], send.at[dst], recv.at[dst], device)

    moves = {}
    moves["x", 1] = forward_x(tok.at[soon], 1, right)
    moves["g", 2] = forward_g(cot.at[soon], 2, left)
    moves["g", 1] = forward_g(cot.at[soon], 1, right)
    moves["x", 2] = forward_x(tok.at[soon], 2, left)
    other = pl.ds(LATE, LATE)
    lates = {
        ("x", 0): remote(tok.at[late], lx.at[other], lx_send.at[0], lx_recv.at[0], partner),
        ("g", 0): remote(cot.at[late], lg.at[other], lg_send.at[0], lg_recv.at[0], partner),
    }
    for move in list(moves.values()) + list(lates.values()):
        move.start()
    w_moves = [
        remote(w, wb.at[1], w_send.at[0], w_recv.at[0], partner),
        remote(w, wn.at[0], w_send.at[1], w_recv.at[1], following),
        remote(w, wn.at[1], w_send.at[2], w_recv.at[2], previous),
    ]
    for move in w_moves:
        move.start()

    acc[...] = jnp.zeros_like(acc)

    def compute(slot, half):
        add_terms(xs[slot], gs[slot], half)

    def add_terms(x, g, half):

        def near(rows, data):
            return lax.dot_general(rows, data, NEAR, preferred_element_type=jnp.float32)

        gate = near(wb[half, 0], x) * width_scale
        upper = near(wb[half, 1], x) * width_scale
        back = near(wb[half, 2], g) * hidden_scale
        sigma = jax.nn.sigmoid(gate)
        swish = gate * sigma
        hidden = (swish * upper).astype(jnp.bfloat16)
        dgate = (back * upper * sigma * (1.0 + gate * (1.0 - sigma))).astype(jnp.bfloat16)
        dupper = (back * swish).astype(jnp.bfloat16)
        acc[half, 0] += jnp.dot(dgate, x, preferred_element_type=jnp.float32)
        acc[half, 1] += jnp.dot(dupper, x, preferred_element_type=jnp.float32)
        acc[half, 2] += jnp.dot(hidden, g, preferred_element_type=jnp.float32)

    def both_halves(first_slot, slots):
        @pl.loop(0, 2 * slots)
        def _(i):
            compute(first_slot + i // 2, 1 - i % 2)

    for copy in local:
        copy.wait()
    compute(0, 0)
    for step in (1, 2, 3):
        r, l = 2 * step - 1, 2 * step
        order = (("x", r), ("g", l), ("g", r), ("x", l))
        for kind, slot in order:
            moves[kind, slot].wait_recv()
            if step < 3:
                target, device = slot + 2, right if slot == r else left
            elif (kind, slot) == ("x", r):
                target, device = 7, right
            elif (kind, slot) == ("g", l):
                target, device = 7, left
            else:
                continue
            if kind == "x":
                moves[kind, target] = forward_x(xs.at[slot], target, device)
            else:
                moves[kind, target] = forward_g(gs.at[slot], target, device)
            moves[kind, target].start()
        if step == 3:
            for kind in ("x", "g"):
                lates[kind, 0].wait_recv()
            for kind, dst, device in (("x", 1, right), ("g", 2, left), ("g", 1, right), ("x", 2, left)):
                lates[kind, dst] = forward_late(kind, 0, dst, device)
                lates[kind, dst].start()
        if step == 1:
            w_moves[0].wait_recv()
            compute(0, 1)
        both_halves(r, 2)
    moves["x", 7].wait_recv()
    moves["g", 7].wait_recv()
    compute(7, 1)

    pieces = [(m, pl.ds(lo, n)) for m in range(3) for lo, n in cuts(units)]
    p_moves = []
    for i, (m, rows) in enumerate(pieces):
        gsend[m, rows] = acc[1, m, rows].astype(LINK)
        p_moves.append(
            remote(gsend.at[m, rows], grecv.at[m, rows], p_send.at[i], p_recv.at[i], partner)
        )
        p_moves[-1].start()
    compute(7, 0)

    def add_late(pair):
        rows = pl.ds(4 * LATE * pair, 4 * LATE)
        add_terms(lx[rows], lg[rows], 0)

    for step in (1, 2, 3):
        r, l = 2 * step - 1, 2 * step
        for kind, slot in (("x", r), ("g", l), ("g", r), ("x", l)):
            lates[kind, slot].wait_recv()
            target, device = slot + 2, right if slot == r else left
            if step == 3:
                if (kind, slot) not in (("x", r), ("g", l)):
                    continue
                target = 7
            lates[kind, target] = forward_late(kind, slot, target, device)
            lates[kind, target].start()
        add_late(step - 1)
    for kind in ("x", "g"):
        lates[kind, 7].wait_recv()
    add_late(3)
    w_moves[1].wait_recv()
    w_moves[2].wait_recv()

    correct_one = 1.0 - 0.9**STEP
    correct_two = 1.0 - 0.95**STEP
    s_moves = []
    detours = range(1, len(pieces), 2)

    def adam(i):
        m, rows = pieces[i]
        p_moves[i].wait_recv()
        grad = (acc[0, m, rows] + grecv[m, rows].astype(jnp.float32)) * scales[m]
        one = 0.9 * fmv[m, rows].astype(jnp.float32) + 0.1 * grad
        two = 0.95 * smv[m, rows].astype(jnp.float32) + 0.05 * grad * grad
        step = one / correct_one / (jnp.sqrt(two / correct_two) + 1e-08)
        acc[0, m, rows] = step
        ssend[m, rows] = step.astype(LINK)
        ends = ((following, last, across), (previous, first, across))
        for j, (device, wraps, relay) in enumerate(ends):
            move = remote(
                ssend.at[m, rows],
                srecv.at[j, m, rows],
                s_send.at[j, i],
                s_recv.at[j, i],
                device,
            )
            s_moves.append(move)
            if i not in detours:
                move.start()
                continue
            pl.when(jnp.logical_not(wraps))(move.start)
            detour = remote(
                ssend.at[m, rows],
                relayed.at[m, rows],
                s_send.at[j, i],
                r_recv.at[i],
                relay,
            )
            pl.when(wraps)(detour.start)

    def relay_on(i, j, device):
        m, rows = pieces[i]
        return remote(
            relayed.at[m, rows], srecv.at[j, m, rows], r_send.at[i], s_recv.at[j, i], device
        )

    def relay(i):
        m, rows = pieces[i]
        for j, (wraps, device) in enumerate(((first, up), (last, down))):

            @pl.when(wraps)
            def _(j=j, device=device):
                remote(
                    relayed.at[m, rows], relayed.at[m, rows], r_send.at[i], r_recv.at[i], across
                ).wait_recv()
                relay_on(i, j, device).start()

    def average(i):
        m, rows = pieces[i]
        s_moves[2 * i].wait_recv()
        s_moves[2 * i + 1].wait_recv()
        f32 = jnp.float32
        steps = acc[0, m, rows] + srecv[0, m, rows].astype(f32) + srecv[1, m, rows].astype(f32)
        rest = wb[0, m, rows].astype(f32) + wn[0, m, rows].astype(f32) + wn[1, m, rows].astype(f32)
        out[m, rows] = 0.99 * rest - 0.1 * steps

    for i in range(len(pieces)):
        adam(i)
    for i in detours:
        relay(i)
    for i in range(len(pieces)):
        average(i)
    for move in list(moves.values()) + list(lates.values()) + w_moves + p_moves + s_moves:
        move.wait_send()

    @pl.when(wraps_round)
    def _():
        for i in detours:
            relay_on(i, 0, across).wait_send()


def on_device(n_blk, n_tp, tokens, cotangent, weights, first_moment, second_moment):
    rows, width = tokens.shape
    units = weights.shape[1]
    shape = (3, units, width)
    bf16, f32 = jnp.bfloat16, jnp.float32
    slots = n_tp // 2
    pieces = 3 * PARTS
    by_kind = [a[0].transpose(1, 0, 2) for a in (weights, first_moment, second_moment)]
    dma = pltpu.SemaphoreType.DMA
    arrays = [pltpu.with_memory_space_constraint(a, pltpu.HBM) for a in (tokens, cotangent, *by_kind)]
    total = pl.pallas_call(
        functools.partial(kernel, n_blk, n_tp, (units * n_tp) ** (-0.5)),
        out_shape=jax.ShapeDtypeStruct(shape, f32),
        in_specs=[pl.BlockSpec(memory_space=pltpu.HBM)] * 5,
        out_specs=pl.BlockSpec(memory_space=pltpu.VMEM),
        scratch_shapes=[
            pltpu.VMEM((slots, rows - LATE, width), bf16),
            pltpu.VMEM((slots, rows - LATE, width), bf16),
            pltpu.VMEM((slots * 2 * LATE, width), bf16),
            pltpu.VMEM((slots * 2 * LATE, width), bf16),
            pltpu.VMEM((2,) + shape, bf16),
            pltpu.VMEM((2,) + shape, bf16),
            pltpu.VMEM(shape, bf16),
            pltpu.VMEM(shape, bf16),
            pltpu.VMEM((2,) + shape, f32),
            pltpu.VMEM(shape, LINK),
            pltpu.VMEM(shape, LINK),
            pltpu.VMEM(shape, LINK),
            pltpu.VMEM((2,) + shape, LINK),
            pltpu.VMEM(shape, LINK),
            dma((7,)),
            dma((slots,)),
            dma((slots,)),
            dma((slots,)),
            dma((slots,)),
            dma((slots,)),
            dma((slots,)),
            dma((slots,)),
            dma((slots,)),
            dma((3,)),
            dma((3,)),
            dma((pieces,)),
            dma((pieces,)),
            dma((2, pieces)),
            dma((2, pieces)),
            dma((pieces,)),
            dma((pieces,)),
        ],
        compiler_params=pltpu.CompilerParams(
            collective_id=0, has_side_effects=True, vmem_limit_bytes=36 << 20
        ),
    )(*arrays)
    return (total / 3.0).transpose(1, 0, 2)[None]


def solution(mesh):
    in_specs = (
        P(("blk", "tp"), None),
        P(("blk", "tp"), None),
        P("blk", "tp", None, None),
        P("blk", "tp", None, None),
        P("blk", "tp", None, None),
    )
    out_specs = P("blk", "tp", None, None)
    return jax.shard_map(
        functools.partial(on_device, mesh.shape["blk"], mesh.shape["tp"]),
        mesh=mesh,
        in_specs=in_specs,
        out_specs=out_specs,
        check_vma=False,
    )
```

```python
import functools

import jax
import jax.numpy as jnp
from jax import lax
from jax.experimental import pallas as pl
from jax.experimental.pallas import tpu as pltpu
from jax.sharding import PartitionSpec as P

STEP = 10
ROW = 8
PARTS = 3
LATE = 32
MESH = pl.DeviceIdType.MESH
LINK = jnp.bfloat16
NEAR = (((1,), (1,)), ((), ()))


def cuts(units):
    size = units // PARTS // 16 * 16
    return [(i * size, size if i < PARTS - 1 else units - i * size) for i in range(PARTS)]


def kernel(
    n_blk,
    n_tp,
    hidden_scale,
    tok,
    cot,
    w,
    fm,
    sm,
    out,
    xs,
    gs,
    lx,
    lg,
    wb,
    wn,
    fmv,
    smv,
    acc,
    gsend,
    grecv,
    ssend,
    srecv,
    relayed,
    local_sem,
    x_send,
    x_recv,
    g_send,
    g_recv,
    lx_send,
    lx_recv,
    lg_send,
    lg_recv,
    w_send,
    w_recv,
    p_send,
    p_recv,
    s_send,
    s_recv,
    r_send,
    r_recv,
):
    b, t = lax.axis_index("blk"), lax.axis_index("tp")
    units, width = w.shape[1], w.shape[2]
    width_scale = width ** (-0.5)
    soon, late = pl.ds(0, tok.shape[0] - LATE), pl.ds(tok.shape[0] - LATE, LATE)
    scales = (width_scale, width_scale, hidden_scale)
    right = {"blk": b, "tp": lax.rem(t + 2, n_tp)}
    left = {"blk": b, "tp": lax.rem(t + n_tp - 2, n_tp)}
    partner = {"blk": b, "tp": t + 1 - 2 * lax.rem(t, 2)}
    following = {"blk": lax.rem(b + 1, n_blk), "tp": t}
    previous = {"blk": lax.rem(b + n_blk - 1, n_blk), "tp": t}

    place = lax.rem(b, ROW)
    last, first = place == ROW - 1, place == 0
    up = {"blk": lax.rem(b + ROW, n_blk), "tp": t}
    down = {"blk": lax.rem(b + n_blk - ROW, n_blk), "tp": t}
    across = {"blk": lax.rem(b + n_blk + ROW - 1 - 2 * place, n_blk), "tp": t}

    def remote(src, dst, send, recv, device):
        return pltpu.make_async_remote_copy(
            src_ref=src,
            dst_ref=dst,
            send_sem=send,
            recv_sem=recv,
            device_id=device,
            device_id_type=MESH,
        )

    local = [
        pltpu.make_async_copy(src, dst, local_sem.at[i])
        for i, (src, dst) in enumerate(
            (
                (tok.at[soon], xs.at[0]),
                (cot.at[soon], gs.at[0]),
                (w, wb.at[0]),
                (fm, fmv),
                (sm, smv),
                (tok.at[late], lx.at[pl.ds(0, LATE)]),
                (cot.at[late], lg.at[pl.ds(0, LATE)]),
            )
        )
    ]
    barrier = pltpu.get_barrier_semaphore()
    for device in (following, previous, right, left, partner):
        pl.semaphore_signal(barrier, inc=1, device_id=device, device_id_type=MESH)
    for copy in local:
        copy.start()
    wraps_round = jnp.logical_or(last, first)

    @pl.when(jnp.logical_not(wraps_round))
    def _():
        pl.semaphore_wait(barrier, 5)

    @pl.when(wraps_round)
    def _():
        for device in (up, down, across):
            pl.semaphore_signal(barrier, inc=1, device_id=device, device_id_type=MESH)
        pl.semaphore_wait(barrier, 8)

    def forward_x(src, dst, device):
        return remote(src, xs.at[dst], x_send.at[dst], x_recv.at[dst], device)

    def forward_g(src, dst, device):
        return remote(src, gs.at[dst], g_send.at[dst], g_recv.at[dst], device)

    def of_slot(slot):
        return pl.ds(2 * LATE * slot, 2 * LATE)

    def forward_late(kind, src, dst, device):
        held, send, recv = (lx, lx_send, lx_recv) if kind == "x" else (lg, lg_send, lg_recv)
        return remote(held.at[of_slot(src)], held.at[of_slot(dst)], send.at[dst], recv.at[dst], device)

    moves = {}
    moves["x", 1] = forward_x(tok.at[soon], 1, right)
    moves["g", 2] = forward_g(cot.at[soon], 2, left)
    moves["g", 1] = forward_g(cot.at[soon], 1, right)
    moves["x", 2] = forward_x(tok.at[soon], 2, left)
    other = pl.ds(LATE, LATE)
    lates = {
        ("x", 0): remote(tok.at[late], lx.at[other], lx_send.at[0], lx_recv.at[0], partner),
        ("g", 0): remote(cot.at[late], lg.at[other], lg_send.at[0], lg_recv.at[0], partner),
    }
    for move in list(moves.values()) + list(lates.values()):
        move.start()
    w_moves = [
        remote(w, wb.at[1], w_send.at[0], w_recv.at[0], partner),
        remote(w, wn.at[0], w_send.at[1], w_recv.at[1], following),
        remote(w, wn.at[1], w_send.at[2], w_recv.at[2], previous),
    ]
    for move in w_moves:
        move.start()

    acc[...] = jnp.zeros_like(acc)

    def compute(slot, half, then=None):
        add_terms(xs[slot], gs[slot], half, then)

    def add_terms(x, g, half, then=None):

        def near(rows, data):
            return lax.dot_general(rows, data, NEAR, preferred_element_type=jnp.float32)

        gate = near(wb[half, 0], x) * width_scale
        upper = near(wb[half, 1], x) * width_scale
        back = near(wb[half, 2], g) * hidden_scale
        sigma = jax.nn.sigmoid(gate)
        swish = gate * sigma
        hidden = (swish * upper).astype(jnp.bfloat16)
        dgate = (back * upper * sigma * (1.0 + gate * (1.0 - sigma))).astype(jnp.bfloat16)
        dupper = (back * swish).astype(jnp.bfloat16)
        for m, (rows, data) in enumerate(((dgate, x), (dupper, x), (hidden, g))):
            acc[half, m] += jnp.dot(rows, data, preferred_element_type=jnp.float32)
            if then is not None:
                then(m)

    def both_halves(first_slot, slots):
        @pl.loop(0, 2 * slots)
        def _(i):
            compute(first_slot + i // 2, 1 - i % 2)

    for copy in local:
        copy.wait()
    compute(0, 0)
    for step in (1, 2, 3):
        r, l = 2 * step - 1, 2 * step
        order = (("x", r), ("g", l), ("g", r), ("x", l))
        for kind, slot in order:
            moves[kind, slot].wait_recv()
            if step < 3:
                target, device = slot + 2, right if slot == r else left
            elif (kind, slot) == ("x", r):
                target, device = 7, right
            elif (kind, slot) == ("g", l):
                target, device = 7, left
            else:
                continue
            if kind == "x":
                moves[kind, target] = forward_x(xs.at[slot], target, device)
            else:
                moves[kind, target] = forward_g(gs.at[slot], target, device)
            moves[kind, target].start()
        if step == 3:
            for kind in ("x", "g"):
                lates[kind, 0].wait_recv()
            for kind, dst, device in (("x", 1, right), ("g", 2, left), ("g", 1, right), ("x", 2, left)):
                lates[kind, dst] = forward_late(kind, 0, dst, device)
                lates[kind, dst].start()
        if step == 1:
            w_moves[0].wait_recv()
            compute(0, 1)
        both_halves(r, 2)
    moves["x", 7].wait_recv()
    moves["g", 7].wait_recv()

    pieces = [(m, pl.ds(lo, n)) for m in range(3) for lo, n in cuts(units)]
    p_moves = []

    def give(of):
        for i, (m, rows) in enumerate(pieces):
            if m != of:
                continue
            gsend[m, rows] = acc[1, m, rows].astype(LINK)
            p_moves.append(
                remote(gsend.at[m, rows], grecv.at[m, rows], p_send.at[i], p_recv.at[i], partner)
            )
            p_moves[-1].start()

    compute(7, 1, give)
    compute(7, 0)

    def add_late(pair, then=None):
        rows = pl.ds(4 * LATE * pair, 4 * LATE)
        add_terms(lx[rows], lg[rows], 0, then)

    for step in (1, 2, 3):
        r, l = 2 * step - 1, 2 * step
        for kind, slot in (("x", r), ("g", l), ("g", r), ("x", l)):
            lates[kind, slot].wait_recv()
            target, device = slot + 2, right if slot == r else left
            if step == 3:
                if (kind, slot) not in (("x", r), ("g", l)):
                    continue
                target = 7
            lates[kind, target] = forward_late(kind, slot, target, device)
            lates[kind, target].start()
        add_late(step - 1)
    for kind in ("x", "g"):
        lates[kind, 7].wait_recv()

    correct_one = 1.0 - 0.9**STEP
    correct_two = 1.0 - 0.95**STEP
    s_moves = []
    detours = (0, 2, 4, 6)

    def adam(i):
        m, rows = pieces[i]
        p_moves[i].wait_recv()
        grad = (acc[0, m, rows] + grecv[m, rows].astype(jnp.float32)) * scales[m]
        one = 0.9 * fmv[m, rows].astype(jnp.float32) + 0.1 * grad
        two = 0.95 * smv[m, rows].astype(jnp.float32) + 0.05 * grad * grad
        step = one / correct_one / (jnp.sqrt(two / correct_two) + 1e-08)
        acc[0, m, rows] = step
        ssend[m, rows] = step.astype(LINK)
        ends = ((following, last, across), (previous, first, across))
        for j, (device, wraps, relay) in enumerate(ends):
            move = remote(
                ssend.at[m, rows],
                srecv.at[j, m, rows],
                s_send.at[j, i],
                s_recv.at[j, i],
                device,
            )
            s_moves.append(move)
            if i not in detours:
                move.start()
                continue
            pl.when(jnp.logical_not(wraps))(move.start)
            detour = remote(
                ssend.at[m, rows],
                relayed.at[m, rows],
                s_send.at[j, i],
                r_recv.at[i],
                relay,
            )
            pl.when(wraps)(detour.start)

    def relay_on(i, j, device):
        m, rows = pieces[i]
        return remote(
            relayed.at[m, rows], srecv.at[j, m, rows], r_send.at[i], s_recv.at[j, i], device
        )

    def relay(i):
        m, rows = pieces[i]
        for j, (wraps, device) in enumerate(((first, up), (last, down))):

            @pl.when(wraps)
            def _(j=j, device=device):
                remote(
                    relayed.at[m, rows], relayed.at[m, rows], r_send.at[i], r_recv.at[i], across
                ).wait_recv()
                relay_on(i, j, device).start()

    def average(i):
        m, rows = pieces[i]
        s_moves[2 * i].wait_recv()
        s_moves[2 * i + 1].wait_recv()
        f32 = jnp.float32
        steps = acc[0, m, rows] + srecv[0, m, rows].astype(f32) + srecv[1, m, rows].astype(f32)
        rest = wb[0, m, rows].astype(f32) + wn[0, m, rows].astype(f32) + wn[1, m, rows].astype(f32)
        out[m, rows] = 0.99 * rest - 0.1 * steps

    def finish(of):
        for i, (m, _) in enumerate(pieces):
            if m == of:
                adam(i)

    add_late(3, finish)
    w_moves[1].wait_recv()
    w_moves[2].wait_recv()
    for i in detours:
        relay(i)
    for i in range(len(pieces)):
        average(i)
    for move in list(moves.values()) + list(lates.values()) + w_moves + p_moves + s_moves:
        move.wait_send()

    @pl.when(wraps_round)
    def _():
        for i in detours:
            relay_on(i, 0, across).wait_send()


def on_device(n_blk, n_tp, tokens, cotangent, weights, first_moment, second_moment):
    rows, width = tokens.shape
    units = weights.shape[1]
    shape = (3, units, width)
    bf16, f32 = jnp.bfloat16, jnp.float32
    slots = n_tp // 2
    pieces = 3 * PARTS
    by_kind = [a[0].transpose(1, 0, 2) for a in (weights, first_moment, second_moment)]
    dma = pltpu.SemaphoreType.DMA
    arrays = [pltpu.with_memory_space_constraint(a, pltpu.HBM) for a in (tokens, cotangent, *by_kind)]
    total = pl.pallas_call(
        functools.partial(kernel, n_blk, n_tp, (units * n_tp) ** (-0.5)),
        out_shape=jax.ShapeDtypeStruct(shape, f32),
        in_specs=[pl.BlockSpec(memory_space=pltpu.HBM)] * 5,
        out_specs=pl.BlockSpec(memory_space=pltpu.VMEM),
        scratch_shapes=[
            pltpu.VMEM((slots, rows - LATE, width), bf16),
            pltpu.VMEM((slots, rows - LATE, width), bf16),
            pltpu.VMEM((slots * 2 * LATE, width), bf16),
            pltpu.VMEM((slots * 2 * LATE, width), bf16),
            pltpu.VMEM((2,) + shape, bf16),
            pltpu.VMEM((2,) + shape, bf16),
            pltpu.VMEM(shape, bf16),
            pltpu.VMEM(shape, bf16),
            pltpu.VMEM((2,) + shape, f32),
            pltpu.VMEM(shape, LINK),
            pltpu.VMEM(shape, LINK),
            pltpu.VMEM(shape, LINK),
            pltpu.VMEM((2,) + shape, LINK),
            pltpu.VMEM(shape, LINK),
            dma((7,)),
            dma((slots,)),
            dma((slots,)),
            dma((slots,)),
            dma((slots,)),
            dma((slots,)),
            dma((slots,)),
            dma((slots,)),
            dma((slots,)),
            dma((3,)),
            dma((3,)),
            dma((pieces,)),
            dma((pieces,)),
            dma((2, pieces)),
            dma((2, pieces)),
            dma((pieces,)),
            dma((pieces,)),
        ],
        compiler_params=pltpu.CompilerParams(
            collective_id=0, has_side_effects=True, vmem_limit_bytes=36 << 20
        ),
    )(*arrays)
    return (total / 3.0).transpose(1, 0, 2)[None]


def solution(mesh):
    in_specs = (
        P(("blk", "tp"), None),
        P(("blk", "tp"), None),
        P("blk", "tp", None, None),
        P("blk", "tp", None, None),
        P("blk", "tp", None, None),
    )
    out_specs = P("blk", "tp", None, None)
    return jax.shard_map(
        functools.partial(on_device, mesh.shape["blk"], mesh.shape["tp"]),
        mesh=mesh,
        in_specs=in_specs,
        out_specs=out_specs,
        check_vma=False,
    )
```
